128 devices in a mesh: chan: 8 (over y, x_hi), strip: 16 (over z, x_lo, core).
Axes of the slice: x: 4 (x_hi: 2, x_lo: 2; x = x_hi * 2 + x_lo), y: 4, z: 4, core: 2. Of those that a mesh axis runs over, the one named last changes fastest.
Arguments:
- wave_field: float32 [2, 16, 1536, 1536], P(None, 'chan', 'strip'), may hold values from -6 to 6
- radial_op: float32 [1536, 1536], replicated, may hold values from -1 to 1, as said below
- coupling: float32 [2, 16, 8], replicated, may hold values from -4 to 4
- couple: int32 [16, 8], replicated, may hold values from 0 to 15
- partner: int32 [16], replicated, may hold values from 0 to 15, as said below
- extent: int32 [16], replicated, may hold values from 384 to 1536, as said below
Outputs:
- first_step: float32 [2, 16, 1536, 1536], P(None, None, 'strip', 'chan')
- second_step: float32 [2, 16, 1536, 1536], P(None, None, 'strip', 'chan')
The draws below stay inside these ranges and needn't reach their ends.
Inputs may be any that keep to these rules, and one draw needn't show every extreme that they name: radial_op is symmetric. partner pairs the channels: partner(partner(c)) == c and partner(c) != c. Each extent is a multiple of 96; some channel has extent 1536 and some 1536 // 4.
All inputs are finite; a program needn't handle non-finite values.
Results may differ from the reference program's by a relative error of at most 0.0003.
Values sent between devices are 32-bit elements; how exact they have to be, the bound alone decides.
No kernel may reach another device: no remote copies, remote signals or barrier semaphores. Data moves between devices by JAX's collectives and lax.ppermute only.
A program may use at most 128 MiB of HBM per device.

```python
import jax
import jax.numpy as jnp
from jax import lax

NR = 1536
CH = 16
MULT = 8


def draw_radial_op(key, part):
    noise = jnp.clip(jax.random.normal(key, (NR, NR), jnp.float32), -6.0, 6.0)
    sym = (noise + noise.T) * (0.35 / jnp.sqrt(2.0 * NR))
    diagonal = jax.random.uniform(jax.random.fold_in(key, 1), (NR,), jnp.float32, -0.5, 0.5)
    return sym + jnp.diag(diagonal)


def draw_partner(key, part):
    order = jax.random.permutation(key, CH).astype(jnp.int32)
    paired = jnp.zeros((CH,), jnp.int32)
    paired = paired.at[order[0::2]].set(order[1::2])
    paired = paired.at[order[1::2]].set(order[0::2])
    return paired


def draw_extent(key, part):
    steps = jax.random.randint(key, (CH,), 0, 13).astype(jnp.int32)
    order = jax.random.permutation(jax.random.fold_in(key, 1), CH).astype(jnp.int32)
    steps = steps.at[order[0]].set(0)
    steps = steps.at[order[1]].set(12)
    return (NR - steps * (NR // 16)).astype(jnp.int32)


def with_ends(array, key, least, largest):
    longest = array.shape.index(max(array.shape))
    spots = []
    for shift in (0, 1):
        where = [jax.random.randint(jax.random.fold_in(key, axis), (), 0, length) for axis, length in enumerate(array.shape)]
        where[longest] = (where[longest] + shift) % array.shape[longest]
        spots.append(tuple(where))
    return array.at[spots[0]].set(least).at[spots[1]].set(largest)


def block_scale(stream_key, shape, pieces, smallest, largest):
    def one(axis_at, blocks):
        steps = jax.random.uniform(jax.random.fold_in(jax.random.fold_in(stream_key, 6), axis_at), (blocks,), jnp.float32, smallest / len(pieces), largest / len(pieces))
        return jnp.repeat(jnp.exp(steps), shape[axis_at] // blocks).reshape((-1,) + (1,) * (len(shape) - axis_at - 1))

    factor_of = one(*pieces[0])
    for cut in pieces[1:]:
        factor_of = factor_of * one(*cut)
    return factor_of


def centred(key, dims, spread, most, cuts=(), dtype=jnp.bfloat16):
    values = jax.random.normal(key, dims, jnp.float32) * spread
    if len(cuts) > 0:
        values = block_scale(key, dims, cuts, -0.22, 0.18) * values
    return jnp.clip(values, min=-most, max=most).astype(dtype)


def setup_inputs(seed: int = 0) -> dict:
    arg_keys = jax.random.split(jax.random.key(seed), 7)
    return {
        "wave_field": centred(arg_keys[0], (2, CH, NR, NR), 1.0, 6.0, ((1, 8), (2, 16)), jnp.float32),
        "radial_op": draw_radial_op(jax.random.fold_in(arg_keys[6], 71), 0),
        "coupling": centred(arg_keys[2], (2, CH, MULT), 0.3, 4.0, (), jnp.float32),
        "couple": with_ends(jax.random.randint(arg_keys[3], (CH, MULT), 0, CH), jax.random.fold_in(arg_keys[3], 1), 0, CH - 1).astype(jnp.int32),
        "partner": draw_partner(jax.random.fold_in(arg_keys[6], 71), 0),
        "extent": draw_extent(jax.random.fold_in(arg_keys[6], 71), 0),
    }


def potentials(row_pos, col_pos, count, orders):
    spacing = 8.0 / count
    first = row_pos.astype(jnp.float32) * spacing
    second = col_pos.astype(jnp.float32) * spacing
    lesser = jnp.minimum(first[:, None], second[None, :])
    greater = jnp.maximum(first[:, None], second[None, :])
    root = jnp.sqrt(greater * greater + 1.0)
    result = []
    for order in range(orders):
        result.append(lesser ** order / root ** (order + 1))
    return result

def reference(wave_field, radial_op, coupling, couple, partner, extent):
    positions = jnp.arange(NR).astype(jnp.int32)
    pots = potentials(positions, positions, NR, MULT)

    def apply(field):
        image = jnp.einsum('ak,pckb->pcab', radial_op, field, precision=lax.Precision.HIGHEST)

        def single(channel):
            total = image[:, channel] + jnp.swapaxes(image[:, partner[channel]], 1, 2)
            real_part = total[0]
            imag_part = total[1]
            for order in range(MULT):
                source = field[:, couple[channel, order]]
                c_real = coupling[0, channel, order]
                c_imag = coupling[1, channel, order]
                real_part = real_part + pots[order] * (c_real * source[0] - c_imag * source[1])
                imag_part = imag_part + pots[order] * (c_real * source[1] + c_imag * source[0])
            live = (positions[:, None] < extent[channel]) & (positions[None, :] < extent[channel])
            return jnp.where(live[None], jnp.stack([real_part, imag_part]), 0.0)
        return jnp.moveaxis(lax.map(single, jnp.arange(CH).astype(jnp.int32)), 0, 1)
    first_step = apply(wave_field)
    second_step = 2.0 * apply(first_step) - wave_field
    return (first_step, second_step)
```

```python
import functools

import jax
import jax.numpy as jnp
from jax import lax
from jax.experimental import pallas as pl
from jax.experimental.pallas import tpu as pltpu
from jax.sharding import PartitionSpec as P

NR = 1536
CH = 16
MULT = 8
DEV = 128
GRP = 8
STR = 16
COLS = 12
LANES = 128
ROWS = 384
WIRE = 4608
EACH = 36


def swap_groups(regs):
    lane = lax.broadcasted_iota(jnp.int32, (8, LANES), 1)
    regs = list(regs)
    for bit in (1, 2, 4, 8):
        upper = (lane & (8 * bit)) != 0
        for i in range(16):
            if i & bit:
                continue
            low, high = regs[i], regs[i | bit]
            regs[i] = jnp.where(upper, pltpu.roll(high, 8 * bit, 1), low)
            regs[i | bit] = jnp.where(upper, high, pltpu.roll(low, LANES - 8 * bit, 1))
    return regs


def row_of(part, y):
    return (y // 4) * 8 + part * 4 + y % 4


def params(mib=48):
    return pltpu.CompilerParams(vmem_limit_bytes=mib << 20)


def cost(flops, moved):
    return pl.CostEstimate(flops=flops, bytes_accessed=moved, transcendentals=0)


def pack_input_kernel(in_ref, out_ref):
    for j in range(3):
        regs = []
        for i in range(16):
            pc, ya = divmod(16 * j + i, COLS)
            regs.append(in_ref[pl.ds(pc * 96 + ya, 8, stride=COLS), :])
        out_ref[pl.ds(j, LANES, stride=3), :] = jnp.concatenate(regs, axis=0).T


def pack_input(wave):
    return pl.pallas_call(
        pack_input_kernel,
        out_shape=jax.ShapeDtypeStruct((WIRE, LANES), jnp.float32),
        grid=(COLS,),
        in_specs=[pl.BlockSpec((ROWS, LANES), lambda i: (0, i))],
        out_specs=pl.BlockSpec((ROWS, LANES), lambda i: (i, 0)),
        compiler_params=params(),
        name="pack_input",
    )(wave)


def order_operator_kernel(in_ref, high_ref, low_ref, held):
    step = pl.program_id(0)

    @pl.when(step < COLS)
    def _():
        for y in range(COLS):
            block = in_ref[pl.ds(y, LANES, stride=COLS), :].T
            held[y, pl.ds(pl.multiple_of(step * LANES, LANES), LANES), :] = block

    @pl.when(step >= COLS)
    def _():
        y = step - COLS
        for ya in range(COLS):
            block = held[y, pl.ds(ya, LANES, stride=COLS), :]
            high = block.astype(jnp.bfloat16)
            high_ref[ya * LANES : (ya + 1) * LANES, :] = high
            low_ref[ya * LANES : (ya + 1) * LANES, :] = (
                block - high.astype(jnp.float32)
            ).astype(jnp.bfloat16)


def order_operator(radial_op):
    out = jax.ShapeDtypeStruct((NR, NR), jnp.bfloat16)
    spec = pl.BlockSpec((NR, LANES), lambda i: (0, jnp.maximum(i - COLS, 0)))
    return pl.pallas_call(
        order_operator_kernel,
        out_shape=(out, out),
        grid=(2 * COLS,),
        in_specs=[pl.BlockSpec((NR, LANES), lambda i: (0, jnp.minimum(i, COLS - 1)))],
        out_specs=(spec, spec),
        scratch_shapes=[pltpu.VMEM((COLS, NR, LANES), jnp.float32)],
        compiler_params=params(),
        cost_estimate=cost(1 << 24, 4 * NR * NR * 2),
        name="order_operator",
    )(radial_op)


def split_terms(tiles_ref, high, low):
    for tile in range(COLS):
        block = tiles_ref[tile]
        upper = block.astype(jnp.bfloat16)
        high[:, tile * LANES : (tile + 1) * LANES] = upper
        low[:, tile * LANES : (tile + 1) * LANES] = (
            block - upper.astype(jnp.float32)
        ).astype(jnp.bfloat16)


def radial_step(step, high, low, op_high_ref, op_low_ref, image_ref, wire_ref):
    op_high = op_high_ref[...]
    image = jnp.dot(high[...], op_high, preferred_element_type=jnp.float32)
    image += jnp.dot(low[...], op_high, preferred_element_type=jnp.float32)
    image += jnp.dot(high[...], op_low_ref[...], preferred_element_type=jnp.float32)
    for half in range(2):
        block = image[:, half * LANES : (half + 1) * LANES]
        image_ref[half] = block
        for j in range(3):
            regs = [block[24 * c + 8 * j : 24 * c + 8 * j + 8, :] for c in range(CH)]
            start = (step * 2 + half) * 3 + j
            wire_ref[pl.ds(start, LANES, stride=EACH), :] = jnp.concatenate(regs, axis=0).T


def first_image_kernel(
    recv_ref, op_high_ref, op_low_ref, field_ref, image_ref, wire_ref, high, low
):
    step = pl.program_id(0)

    @pl.when(step == 0)
    def _():
        for y in range(COLS):
            for j in range(3):
                regs = swap_groups(
                    recv_ref[pl.ds(s * EACH + y * 3 + j, 8, stride=STR * EACH), :]
                    for s in range(STR)
                )
                for i in range(16):
                    pc, ya = divmod(16 * j + i, COLS)
                    start = (pc % 2) * 24 + row_of(pc // 2, y)
                    field_ref[ya, pl.ds(start, 8, stride=48), :] = regs[i]
        split_terms(field_ref, high, low)

    radial_step(step, high, low, op_high_ref, op_low_ref, image_ref, wire_ref)


TILES = jax.ShapeDtypeStruct((COLS, ROWS, LANES), jnp.float32)
SENT = jax.ShapeDtypeStruct((WIRE, LANES), jnp.float32)
SMEM = pl.BlockSpec(memory_space=pltpu.SMEM)


def whole(shape):
    return pl.BlockSpec(shape, lambda i: (0,) * len(shape))


OP_SPEC = pl.BlockSpec((NR, 2 * LANES), lambda i: (0, i))
PAIR_SPEC = pl.BlockSpec((2, ROWS, LANES), lambda i: (i, 0, 0))
FLOPS = 2 * 3 * ROWS * NR * NR


def first_image(recv, op_high, op_low):
    return pl.pallas_call(
        first_image_kernel,
        out_shape=(TILES, TILES, SENT),
        grid=(COLS // 2,),
        in_specs=[whole((WIRE, LANES)), OP_SPEC, OP_SPEC],
        out_specs=(whole(TILES.shape), PAIR_SPEC, whole(SENT.shape)),
        scratch_shapes=[
            pltpu.VMEM((ROWS, NR), jnp.bfloat16),
            pltpu.VMEM((ROWS, NR), jnp.bfloat16),
        ],
        compiler_params=params(),
        cost_estimate=cost(FLOPS, 20 << 20),
        name="first_image",
    )(recv, op_high, op_low)


def position_of(step, device):
    lane = lax.broadcasted_iota(jnp.int32, (24, LANES), 1)
    row = lax.broadcasted_iota(jnp.int32, (24, LANES), 0)
    return 12 * lane + step, 12 * device + (row // 8) * 4 + row % 4


def couple_kernel(device_ref, coupling_ref, couple_ref, field_ref, image_ref, out_ref, turned):
    step = pl.program_id(0)
    a, b = position_of(step, device_ref[0])
    first = a.astype(jnp.float32) * (8.0 / NR)
    second = b.astype(jnp.float32) * (8.0 / NR)
    greater = jnp.maximum(first, second)
    inverse = 1.0 / jnp.sqrt(greater * greater + 1.0)
    ratio = jnp.minimum(first, second) * inverse
    row = lax.broadcasted_iota(jnp.int32, (8, LANES), 0)
    sign = jnp.where(row < 4, -1.0, 1.0)
    for c in range(CH):
        for t in range(3):
            block = field_ref[0, c, 8 * t : 8 * t + 8, :]
            turned[c, 8 * t : 8 * t + 8, :] = pltpu.roll(block, 4, 0) * sign

    @pl.loop(0, CH)
    def _(c):
        total = jnp.zeros((24, LANES), jnp.float32)
        for order in reversed(range(MULT)):
            source = couple_ref[c, order]
            term = coupling_ref[0, c, order] * field_ref[0, source]
            term += coupling_ref[1, c, order] * turned[source]
            total = total * ratio + term
        out_ref[0, c] = image_ref[0, c] + total * inverse


def couple_terms(device, coupling, couple, field, image):
    shape = (COLS, CH, 24, LANES)
    spec = pl.BlockSpec((1,) + shape[1:], lambda i: (i, 0, 0, 0))
    out = pl.pallas_call(
        couple_kernel,
        out_shape=jax.ShapeDtypeStruct(shape, jnp.float32),
        grid=(COLS,),
        in_specs=[SMEM, SMEM, SMEM, spec, spec],
        out_specs=spec,
        scratch_shapes=[pltpu.VMEM((CH, 24, LANES), jnp.float32)],
        compiler_params=params(),
        cost_estimate=cost(1 << 28, 8 << 20),
        name="couple_terms",
    )(device, coupling, couple, field.reshape(shape), image.reshape(shape))
    return out.reshape(TILES.shape)


def unpack_mirror(recv_ref, mirror, block):
    for y in range(COLS):
        for j in range(3):
            block[...] = recv_ref[pl.ds(y * 3 + j, LANES, stride=EACH), :].T
            for part in range(2):
                for k in range(4):
                    mirror[4 * j + k, pl.ds(row_of(part, y), CH, stride=24), :] = block[
                        pl.ds(part * 4 + k, CH, stride=8), :
                    ]


def live_sum(tile, c, device_ref, partner_ref, extent_ref, direct_ref, mirror):
    a, b = position_of(tile, device_ref[0])
    extent = extent_ref[c]
    here = pl.ds(pl.multiple_of(c * 24, 8), 24)
    there = pl.ds(pl.multiple_of(partner_ref[c] * 24, 8), 24)
    total = direct_ref[tile, here, :] + mirror[tile, there, :]
    return here, jnp.where((a < extent) & (b < extent), total, 0.0)


def pack_output(tiles_ref, wire_ref):
    for tile in range(COLS):
        for t in range(3):
            regs = swap_groups(
                tiles_ref[tile, 24 * c + 8 * t : 24 * c + 8 * t + 8, :] for c in range(CH)
            )
            for s in range(STR):
                start = s * 288 + tile * 24 + t * 8
                wire_ref[start : start + 8, :] = regs[s]


def second_image_kernel(
    device_ref,
    partner_ref,
    extent_ref,
    recv_ref,
    direct_ref,
    op_high_ref,
    op_low_ref,
    field_ref,
    image_ref,
    wire_ref,
    output_ref,
    high,
    low,
    mirror,
    block,
):
    step = pl.program_id(0)

    @pl.when(step == 0)
    def _():
        unpack_mirror(recv_ref, mirror, block)

        @pl.loop(0, COLS)
        def _(tile):
            @pl.loop(0, CH)
            def _(c):
                here, total = live_sum(
                    tile, c, device_ref, partner_ref, extent_ref, direct_ref, mirror
                )
                field_ref[tile, here, :] = total

        split_terms(field_ref, high, low)
        pack_output(field_ref, output_ref)

    radial_step(step, high, low, op_high_ref, op_low_ref, image_ref, wire_ref)


def second_image(device, partner, extent, recv, direct, op_high, op_low):
    return pl.pallas_call(
        second_image_kernel,
        out_shape=(TILES, TILES, SENT, SENT),
        grid=(COLS // 2,),
        in_specs=[
            SMEM,
            SMEM,
            SMEM,
            whole(SENT.shape),
            whole(TILES.shape),
            OP_SPEC,
            OP_SPEC,
        ],
        out_specs=(whole(TILES.shape), PAIR_SPEC, whole(SENT.shape), whole(SENT.shape)),
        scratch_shapes=[
            pltpu.VMEM((ROWS, NR), jnp.bfloat16),
            pltpu.VMEM((ROWS, NR), jnp.bfloat16),
            pltpu.VMEM(TILES.shape, jnp.float32),
            pltpu.VMEM((LANES, LANES), jnp.float32),
        ],
        compiler_params=params(),
        cost_estimate=cost(FLOPS, 25 << 20),
        name="second_image",
    )(device, partner, extent, recv, direct, op_high, op_low)


def second_vector_kernel(
    device_ref,
    partner_ref,
    extent_ref,
    recv_ref,
    direct_ref,
    field_ref,
    output_ref,
    mirror,
    result,
    block,
):
    unpack_mirror(recv_ref, mirror, block)

    @pl.loop(0, COLS)
    def _(tile):
        @pl.loop(0, CH)
        def _(c):
            here, total = live_sum(
                tile, c, device_ref, partner_ref, extent_ref, direct_ref, mirror
            )
            result[tile, here, :] = 2.0 * total - field_ref[tile, here, :]

    pack_output(result, output_ref)


def second_vector(device, partner, extent, recv, direct, field):
    return pl.pallas_call(
        second_vector_kernel,
        out_shape=SENT,
        grid=(1,),
        in_specs=[
            SMEM,
            SMEM,
            SMEM,
            whole(SENT.shape),
            whole(TILES.shape),
            whole(TILES.shape),
        ],
        out_specs=whole(SENT.shape),
        scratch_shapes=[
            pltpu.VMEM(TILES.shape, jnp.float32),
            pltpu.VMEM(TILES.shape, jnp.float32),
            pltpu.VMEM((LANES, LANES), jnp.float32),
        ],
        compiler_params=params(),
        cost_estimate=cost(1 << 24, 10 << 20),
        name="second_vector",
    )(device, partner, extent, recv, direct, field)


def place_output_kernel(recv_ref, out_ref, rows, left, right):
    part = pl.program_id(0)
    for ya in range(COLS):
        for s in range(STR):
            for t in range(3):
                start = s * 288 + ya * 24 + t * 8
                block = recv_ref[start : start + 8, :]
                block = jnp.where(part == 0, block[:4], block[4:])
                rows[12 * s + 4 * t : 12 * s + 4 * t + 4, :] = block
        turned = rows[...].T
        left[pl.ds(ya, LANES, stride=COLS), :] = turned[:, :LANES]
        right[pl.ds(ya, LANES, stride=COLS), :] = turned[:, LANES:]
    out_ref[0, :, :LANES] = left[...]
    out_ref[0, :, LANES:] = right[:, :64]


def place_output(recv):
    out = pl.pallas_call(
        place_output_kernel,
        out_shape=jax.ShapeDtypeStruct((2, NR, 192), jnp.float32),
        grid=(2,),
        in_specs=[whole(SENT.shape)],
        out_specs=pl.BlockSpec((1, NR, 192), lambda i: (i, 0, 0)),
        scratch_shapes=[
            pltpu.VMEM((256, LANES), jnp.float32),
            pltpu.VMEM((NR, LANES), jnp.float32),
            pltpu.VMEM((NR, LANES), jnp.float32),
        ],
        compiler_params=params(),
        cost_estimate=cost(1 << 24, 5 << 20),
        name="place_output",
    )(recv)
    return out.reshape(2, CH, 96, 192)


def exchange_all(sent):
    sent = sent.reshape(DEV, 9, 4, LANES)
    recv = lax.all_to_all(sent, ("chan", "strip"), 0, 0, tiled=True)
    return recv.reshape(WIRE, LANES)


def exchange_strip(sent):
    sent = sent.reshape(STR, WIRE // STR, LANES)
    return lax.all_to_all(sent, "strip", 0, 0, tiled=True).reshape(WIRE, LANES)


def local(wave_field, radial_op, coupling, couple, partner, extent):
    device = (lax.axis_index("chan") * STR + lax.axis_index("strip")).reshape(1)
    op_high, op_low = order_operator(radial_op)
    recv = exchange_all(pack_input(wave_field.reshape(ROWS, NR)))
    field, image, sent = first_image(recv, op_high, op_low)
    recv = exchange_all(sent)
    direct = couple_terms(device, coupling, couple, field, image)
    first, image, sent, output = second_image(
        device, partner, extent, recv, direct, op_high, op_low
    )
    recv = exchange_all(sent)
    direct = couple_terms(device, coupling, couple, first, image)
    first_step = place_output(exchange_strip(output))
    output = second_vector(device, partner, extent, recv, direct, field)
    second_step = place_output(exchange_strip(output))
    return (first_step, second_step)


def solution(mesh):
    placed = (P(None, "chan", "strip", None), P(), P(), P(), P(), P())
    return jax.shard_map(
        local,
        mesh=mesh,
        in_specs=placed,
        out_specs=(P(None, None, "strip", "chan"), P(None, None, "strip", "chan")),
        check_vma=False,
    )
```

```python
import functools

import jax
import jax.numpy as jnp
from jax import lax
from jax.experimental import pallas as pl
from jax.experimental.pallas import tpu as pltpu
from jax.sharding import PartitionSpec as P

NR = 1536
CH = 16
MULT = 8
DEV = 128
GRP = 8
STR = 16
COLS = 12
LANES = 128
ROWS = 384
WIRE = 4608
EACH = 36


TILES = pltpu.HBM((COLS, ROWS, LANES), jnp.float32)
SENT = pltpu.HBM((WIRE, LANES), jnp.float32)
SMEM = pl.BlockSpec(memory_space=pltpu.SMEM)
HBM = pl.BlockSpec(memory_space=pltpu.HBM)
VMEM = pl.BlockSpec(memory_space=pltpu.VMEM)
SENT_SPEC = pl.BlockSpec((WIRE, LANES), lambda i: (0, 0))
TILES_SPEC = pl.BlockSpec((COLS, ROWS, LANES), lambda i: (0, 0, 0))
HELD = pltpu.VMEM((COLS, ROWS, LANES), jnp.float32)
TURN = 4
OP_SPEC = pl.BlockSpec((TURN, NR, LANES), lambda i: (i, 0, 0))
IMAGE_SPEC = pl.BlockSpec((TURN, ROWS, LANES), lambda i: (i, 0, 0))
FLOPS = 2 * 3 * ROWS * NR * NR


def swap_groups(regs):
    lane = lax.broadcasted_iota(jnp.int32, (8, LANES), 1)
    regs = list(regs)
    for bit in (1, 2, 4, 8):
        upper = (lane & (8 * bit)) != 0
        for i in range(16):
            if i & bit:
                continue
            low, high = regs[i], regs[i | bit]
            regs[i] = jnp.where(upper, pltpu.roll(high, 8 * bit, 1), low)
            regs[i | bit] = jnp.where(upper, high, pltpu.roll(low, LANES - 8 * bit, 1))
    return regs


def row_of(part, y):
    return (y // 4) * 8 + part * 4 + y % 4


def params(mib=20):
    return pltpu.CompilerParams(vmem_limit_bytes=mib << 20)


def hbm(*arrays):
    return [pltpu.with_memory_space_constraint(x, pltpu.HBM) for x in arrays]


def cost(flops, moved):
    return pl.CostEstimate(flops=flops, bytes_accessed=moved, transcendentals=0)


def pack_input_kernel(in_ref, out_ref):
    for tile in range(COLS):
        lanes = slice(tile * LANES, (tile + 1) * LANES)
        for j in range(3):
            block = in_ref[j * LANES : (j + 1) * LANES, lanes]
            out_ref[pl.ds(tile * ROWS + j, LANES, stride=3), :] = block.T


def pack_input(wave):
    return pl.pallas_call(
        pack_input_kernel,
        out_shape=SENT,
        grid=(1,),
        in_specs=[pl.BlockSpec((ROWS, NR), lambda i: (0, 0))],
        out_specs=SENT_SPEC,
        compiler_params=params(12),
        name="pack_input",
    )(*hbm(wave))


def order_operator_kernel(in_ref, high_ref, low_ref, held):
    step = pl.program_id(0)

    @pl.when(step < COLS)
    def _():
        for y in range(COLS):
            block = in_ref[pl.ds(y, LANES, stride=COLS), :].T
            held[y, pl.ds(pl.multiple_of(step * LANES, LANES), LANES), :] = block

    @pl.when(step >= COLS)
    def _():
        y = step - COLS
        for ya in range(COLS):
            block = held[y, pl.ds(ya, LANES, stride=COLS), :]
            high = block.astype(jnp.bfloat16)
            rows = slice(ya * LANES, (ya + 1) * LANES)
            high_ref[0, rows, :] = high
            low_ref[0, rows, :] = (block - high.astype(jnp.float32)).astype(jnp.bfloat16)


def order_operator(radial_op):
    out = pltpu.HBM((COLS, NR, LANES), jnp.bfloat16)
    spec = pl.BlockSpec((1, NR, LANES), lambda i: (jnp.maximum(i - COLS, 0), 0, 0))
    return pl.pallas_call(
        order_operator_kernel,
        out_shape=(out, out),
        grid=(2 * COLS,),
        in_specs=[pl.BlockSpec((NR, LANES), lambda i: (0, jnp.minimum(i, COLS - 1)))],
        out_specs=(spec, spec),
        scratch_shapes=[pltpu.VMEM((COLS, NR, LANES), jnp.float32)],
        compiler_params=params(),
        cost_estimate=cost(1 << 24, 4 * NR * NR * 2),
        name="order_operator",
    )(*hbm(radial_op))


def split_terms(tiles_ref, high, low):
    for tile in range(COLS):
        block = tiles_ref[tile]
        upper = block.astype(jnp.bfloat16)
        high[:, tile * LANES : (tile + 1) * LANES] = upper
        low[:, tile * LANES : (tile + 1) * LANES] = (
            block - upper.astype(jnp.float32)
        ).astype(jnp.bfloat16)


def radial_step(step, high, low, op_high_ref, op_low_ref, image_ref, wire_ref):
    op_high = jnp.concatenate([op_high_ref[i] for i in range(TURN)], axis=1)
    op_low = jnp.concatenate([op_low_ref[i] for i in range(TURN)], axis=1)
    image = jnp.dot(high[...], op_high, preferred_element_type=jnp.float32)
    image += jnp.dot(low[...], op_high, preferred_element_type=jnp.float32)
    image += jnp.dot(high[...], op_low, preferred_element_type=jnp.float32)
    for i in range(TURN):
        block = image[:, i * LANES : (i + 1) * LANES]
        image_ref[i] = block
        for j in range(3):
            regs = [block[24 * c + 8 * j : 24 * c + 8 * j + 8, :] for c in range(CH)]
            start = (step * TURN + i) * 3 + j
            wire_ref[pl.ds(start, LANES, stride=EACH), :] = jnp.concatenate(regs, axis=0).T


def unpack_input(recv_ref, field_ref, held):
    for s in range(STR):
        for j in range(3):
            rows = [
                recv_ref[pl.ds(s * EACH + y * 3 + j, 8, stride=STR * EACH), :]
                for y in range(COLS)
            ]
            start = s * ROWS + j * LANES
            held[start : start + LANES, :96] = jnp.concatenate(rows, axis=0).T
    for pc in range(4):
        for ya in range(COLS):
            rows = [
                held[pl.ds(s * ROWS + pc * 96 + ya, 8, stride=COLS), :] for s in range(STR)
            ]
            block = jnp.concatenate(rows, axis=0).T
            for y in range(COLS):
                start = (pc % 2) * 24 + row_of(pc // 2, y)
                field_ref[ya, pl.ds(start, 8, stride=48), :] = block[8 * y : 8 * y + 8, :]


def first_image_kernel(
    recv_ref,
    op_high_ref,
    op_low_ref,
    field_ref,
    image_ref,
    wire_ref,
    high,
    low,
    held,
    field,
    sem,
):
    step = pl.program_id(0)
    keep = pltpu.make_async_copy(field, field_ref, sem)

    @pl.when(step == 0)
    def _():
        unpack_input(recv_ref, field, held)
        keep.start()
        split_terms(field, high, low)

    radial_step(step, high, low, op_high_ref, op_low_ref, image_ref, wire_ref)

    @pl.when(step == COLS // TURN - 1)
    def _():
        keep.wait()


def first_image(recv, op_high, op_low):
    return pl.pallas_call(
        first_image_kernel,
        out_shape=(TILES, TILES, SENT),
        grid=(COLS // TURN,),
        in_specs=[VMEM, OP_SPEC, OP_SPEC],
        out_specs=(HBM, IMAGE_SPEC, SENT_SPEC),
        scratch_shapes=[
            pltpu.VMEM((ROWS, NR), jnp.bfloat16),
            pltpu.VMEM((ROWS, NR), jnp.bfloat16),
            pltpu.VMEM((STR * ROWS, LANES), jnp.float32),
            HELD,
            pltpu.SemaphoreType.DMA,
        ],
        compiler_params=params(32),
        cost_estimate=cost(FLOPS, 20 << 20),
        name="first_image",
    )(recv, *hbm(op_high, op_low))


def position_of(step, device):
    lane = lax.broadcasted_iota(jnp.int32, (24, LANES), 1)
    row = lax.broadcasted_iota(jnp.int32, (24, LANES), 0)
    return 12 * lane + step, 12 * device + (row // 8) * 4 + row % 4


def couple_kernel(device_ref, coupling_ref, couple_ref, field_ref, image_ref, out_ref, turned):
    step = pl.program_id(0)
    a, b = position_of(step, device_ref[0])
    first = a.astype(jnp.float32) * (8.0 / NR)
    second = b.astype(jnp.float32) * (8.0 / NR)
    greater = jnp.maximum(first, second)
    inverse = 1.0 / jnp.sqrt(greater * greater + 1.0)
    ratio = jnp.minimum(first, second) * inverse
    row = lax.broadcasted_iota(jnp.int32, (8, LANES), 0)
    sign = jnp.where(row < 4, -1.0, 1.0)
    for c in range(CH):
        for t in range(3):
            block = field_ref[0, c, 8 * t : 8 * t + 8, :]
            turned[c, 8 * t : 8 * t + 8, :] = pltpu.roll(block, 4, 0) * sign

    @pl.loop(0, CH)
    def _(c):
        total = jnp.zeros((24, LANES), jnp.float32)
        for order in reversed(range(MULT)):
            source = couple_ref[c, order]
            term = coupling_ref[0, c, order] * field_ref[0, source]
            term += coupling_ref[1, c, order] * turned[source]
            total = total * ratio + term
        out_ref[0, c] = image_ref[0, c] + total * inverse


def couple_terms(device, coupling, couple, field, image):
    shape = (COLS, CH, 24, LANES)
    spec = pl.BlockSpec((1,) + shape[1:], lambda i: (i, 0, 0, 0))
    out = pl.pallas_call(
        couple_kernel,
        out_shape=pltpu.HBM(shape, jnp.float32),
        grid=(COLS,),
        in_specs=[SMEM, SMEM, SMEM, spec, spec],
        out_specs=spec,
        scratch_shapes=[pltpu.VMEM((CH, 24, LANES), jnp.float32)],
        compiler_params=params(6),
        cost_estimate=cost(1 << 28, 8 << 20),
        name="couple_terms",
    )(device, coupling, couple, *hbm(field.reshape(shape), image.reshape(shape)))
    return out.reshape(TILES.shape)


def unpack_mirror(recv_ref, mirror, block):
    for y in range(COLS):
        for j in range(3):
            block[...] = recv_ref[pl.ds(y * 3 + j, LANES, stride=EACH), :].T
            for part in range(2):
                for k in range(4):
                    mirror[4 * j + k, pl.ds(row_of(part, y), CH, stride=24), :] = block[
                        pl.ds(part * 4 + k, CH, stride=8), :
                    ]


def live_sums(pair, device_ref, partner_ref, extent_ref, direct_ref, mirror, use):
    here = pl.ds(pl.multiple_of(pair * 48, 16), 48)
    lane, b = position_of(0, device_ref[0])
    for tile in range(COLS):
        rows = []
        for c in range(2):
            channel = pair * 2 + c
            extent = extent_ref[channel]
            there = pl.ds(pl.multiple_of(partner_ref[channel] * 24, 8), 24)
            live = (lane < extent - tile) & (b < extent)
            own = pl.ds(pl.multiple_of(channel * 24, 8), 24)
            total = direct_ref[tile, own, :] + mirror[tile, there, :]
            rows.append(jnp.where(live, total, 0.0))
        use(tile, here, jnp.concatenate(rows, axis=0))


def second_image_kernel(
    device_ref,
    partner_ref,
    extent_ref,
    recv_ref,
    direct_ref,
    op_high_ref,
    op_low_ref,
    field_ref,
    image_ref,
    wire_ref,
    high,
    low,
    mirror,
    block,
    direct,
    field,
    sems,
):
    step = pl.program_id(0)
    fetch = pltpu.make_async_copy(direct_ref, direct, sems.at[0])
    keep = pltpu.make_async_copy(field, field_ref, sems.at[1])

    @pl.when(step == 0)
    def _():
        fetch.start()
        unpack_mirror(recv_ref, mirror, block)
        fetch.wait()

        def use(tile, here, total):
            field[tile, here, :] = total
            lanes = slice(tile * LANES, (tile + 1) * LANES)
            upper = total.astype(jnp.bfloat16)
            high[here, lanes] = upper
            low[here, lanes] = (total - upper.astype(jnp.float32)).astype(jnp.bfloat16)

        @pl.loop(0, CH // 2)
        def _(pair):
            live_sums(pair, device_ref, partner_ref, extent_ref, direct, mirror, use)

        keep.start()

    radial_step(step, high, low, op_high_ref, op_low_ref, image_ref, wire_ref)

    @pl.when(step == COLS // TURN - 1)
    def _():
        keep.wait()


def second_image(device, partner, extent, recv, direct, op_high, op_low):
    return pl.pallas_call(
        second_image_kernel,
        out_shape=(TILES, TILES, SENT),
        grid=(COLS // TURN,),
        in_specs=[SMEM, SMEM, SMEM, VMEM, HBM, OP_SPEC, OP_SPEC],
        out_specs=(HBM, IMAGE_SPEC, SENT_SPEC),
        scratch_shapes=[
            pltpu.VMEM((ROWS, NR), jnp.bfloat16),
            pltpu.VMEM((ROWS, NR), jnp.bfloat16),
            HELD,
            pltpu.VMEM((LANES, LANES), jnp.float32),
            HELD,
            HELD,
            pltpu.SemaphoreType.DMA((2,)),
        ],
        compiler_params=params(36),
        cost_estimate=cost(FLOPS, 25 << 20),
        name="second_image",
    )(device, partner, extent, recv, *hbm(direct, op_high, op_low))


def pack_first_kernel(field_ref, wire_ref):
    for tile in range(COLS):
        for k in range(3):
            block = field_ref[tile, k * LANES : (k + 1) * LANES, :].T
            for s in range(STR):
                start = s * 288 + k * 96 + tile
                wire_ref[pl.ds(start, 8, stride=COLS), :] = block[8 * s : 8 * s + 8, :]


def pack_first(field):
    return pl.pallas_call(
        pack_first_kernel,
        out_shape=SENT,
        grid=(1,),
        in_specs=[TILES_SPEC],
        out_specs=SENT_SPEC,
        compiler_params=params(12),
        cost_estimate=cost(1 << 24, 5 << 20),
        name="pack_first",
    )(*hbm(field))


def place_first_kernel(recv_ref, out_ref, rows):
    for s in range(STR):
        for k in range(3):
            start = s * 288 + k * 96
            block = recv_ref[start : start + 96, :].T
            for i in range(16):
                c, t = divmod(16 * k + i, 3)
                for part in range(2):
                    at = 8 * i + 4 * part
                    rows[part * CH + c, 12 * s + 4 * t : 12 * s + 4 * t + 4, :] = block[
                        at : at + 4, :
                    ]
    for i in range(2 * CH):
        out_ref[i] = rows[i].T


def place_first(recv):
    out = pl.pallas_call(
        place_first_kernel,
        out_shape=jax.ShapeDtypeStruct((2 * CH, 96, 192), jnp.float32),
        grid=(1,),
        in_specs=[SENT_SPEC],
        out_specs=pl.BlockSpec((2 * CH, 96, 192), lambda i: (0, 0, 0)),
        scratch_shapes=[pltpu.VMEM((2 * CH, 192, 96), jnp.float32)],
        compiler_params=params(24),
        cost_estimate=cost(1 << 24, 5 << 20),
        name="place_first",
    )(*hbm(recv))
    return out.reshape(2, CH, 96, 192)


def second_vector_kernel(
    device_ref,
    partner_ref,
    extent_ref,
    recv_ref,
    direct_ref,
    field_ref,
    output_ref,
    mirror,
    result,
    block,
):
    unpack_mirror(recv_ref, mirror, block)

    def keep(tile, here, total):
        result[tile, here, :] = 2.0 * total - field_ref[tile, here, :]

    @pl.loop(0, CH // 2)
    def _(pair):
        live_sums(pair, device_ref, partner_ref, extent_ref, direct_ref, mirror, keep)

    for tile in range(COLS):
        for t in range(3):
            regs = swap_groups(
                result[tile, 24 * c + 8 * t : 24 * c + 8 * t + 8, :] for c in range(CH)
            )
            for s in range(STR):
                start = s * 288 + tile * 24 + t * 8
                output_ref[start : start + 8, :] = regs[s]


def second_vector(device, partner, extent, recv, direct, field):
    return pl.pallas_call(
        second_vector_kernel,
        out_shape=SENT,
        grid=(1,),
        in_specs=[SMEM, SMEM, SMEM, VMEM, TILES_SPEC, TILES_SPEC],
        out_specs=SENT_SPEC,
        scratch_shapes=[HELD, HELD, pltpu.VMEM((LANES, LANES), jnp.float32)],
        compiler_params=params(32),
        cost_estimate=cost(1 << 24, 10 << 20),
        name="second_vector",
    )(device, partner, extent, recv, *hbm(direct, field))


def place_output_kernel(recv_ref, out_ref, rows, left, right):
    part = pl.program_id(0)
    for ya in range(COLS):
        for s in range(STR):
            for t in range(3):
                start = s * 288 + ya * 24 + t * 8
                block = recv_ref[start : start + 8, :]
                block = jnp.where(part == 0, block[:4], block[4:])
                rows[12 * s + 4 * t : 12 * s + 4 * t + 4, :] = block
        turned = rows[...].T
        left[pl.ds(ya, LANES, stride=COLS), :] = turned[:, :LANES]
        right[pl.ds(ya, LANES, stride=COLS), :] = turned[:, LANES:]
    out_ref[0, :, :LANES] = left[...]
    out_ref[0, :, LANES:] = right[:, :64]


def place_output(recv):
    out = pl.pallas_call(
        place_output_kernel,
        out_shape=jax.ShapeDtypeStruct((2, NR, 192), jnp.float32),
        grid=(2,),
        in_specs=[VMEM],
        out_specs=pl.BlockSpec((1, NR, 192), lambda i: (i, 0, 0)),
        scratch_shapes=[
            pltpu.VMEM((256, LANES), jnp.float32),
            pltpu.VMEM((NR, LANES), jnp.float32),
            pltpu.VMEM((NR, LANES), jnp.float32),
        ],
        compiler_params=params(20),
        cost_estimate=cost(1 << 24, 5 << 20),
        name="place_output",
    )(recv)
    return out.reshape(2, CH, 96, 192)


def exchange_all(sent):
    sent = sent.reshape(DEV, 9, 4, LANES)
    recv = lax.all_to_all(sent, ("chan", "strip"), 0, 0, tiled=True)
    return recv.reshape(WIRE, LANES)


def exchange_strip(sent):
    sent = sent.reshape(STR, WIRE // STR, LANES)
    return lax.all_to_all(sent, "strip", 0, 0, tiled=True).reshape(WIRE, LANES)


def local(wave_field, radial_op, coupling, couple, partner, extent):
    device = (lax.axis_index("chan") * STR + lax.axis_index("strip")).reshape(1)
    op_high, op_low = order_operator(radial_op)
    recv = exchange_all(pack_input(wave_field.reshape(ROWS, NR)))
    field, image, sent = first_image(recv, op_high, op_low)
    recv = exchange_all(sent)
    direct = couple_terms(device, coupling, couple, field, image)
    first, image, sent = second_image(
        device, partner, extent, recv, direct, op_high, op_low
    )
    recv = exchange_all(sent)
    direct = couple_terms(device, coupling, couple, first, image)
    first_step = place_first(exchange_strip(pack_first(first)))
    output = second_vector(device, partner, extent, recv, direct, field)
    second_step = place_output(exchange_strip(output))
    return (first_step, second_step)


def solution(mesh):
    placed = (P(None, "chan", "strip", None), P(), P(), P(), P(), P())
    return jax.shard_map(
        local,
        mesh=mesh,
        in_specs=placed,
        out_specs=(P(None, None, "strip", "chan"), P(None, None, "strip", "chan")),
        check_vma=False,
    )
```

```python
import functools

import jax
import jax.numpy as jnp
from jax import lax
from jax.experimental import pallas as pl
from jax.experimental.pallas import tpu as pltpu
from jax.sharding import PartitionSpec as P

NR = 1536
CH = 16
MULT = 8
DEV = 128
GRP = 8
STR = 16
COLS = 12
LANES = 128
ROWS = 384
WIRE = 4608
EACH = 36


TILES = pltpu.HBM((COLS, ROWS, LANES), jnp.float32)
SENT = pltpu.HBM((WIRE, LANES), jnp.float32)
SMEM = pl.BlockSpec(memory_space=pltpu.SMEM)
HBM = pl.BlockSpec(memory_space=pltpu.HBM)
VMEM = pl.BlockSpec(memory_space=pltpu.VMEM)
SENT_SPEC = pl.BlockSpec((WIRE, LANES), lambda i: (0, 0))
TILES_SPEC = pl.BlockSpec((COLS, ROWS, LANES), lambda i: (0, 0, 0))
HELD = pltpu.VMEM((COLS, ROWS, LANES), jnp.float32)
TURN = 4
TURNS = COLS // TURN
PRODUCT_SCRATCH = [
    pltpu.VMEM((ROWS, NR), jnp.bfloat16),
    pltpu.VMEM((ROWS, NR), jnp.bfloat16),
    pltpu.VMEM((COLS, NR, LANES), jnp.bfloat16),
    pltpu.VMEM((COLS, NR, LANES), jnp.bfloat16),
    HELD,
    pltpu.VMEM((WIRE, LANES), jnp.float32),
    pltpu.SemaphoreType.DMA((2 * TURNS,)),
    pltpu.SemaphoreType.DMA((TURNS + 1,)),
]
FLOPS = 2 * 3 * ROWS * NR * NR


def swap_groups(regs):
    lane = lax.broadcasted_iota(jnp.int32, (8, LANES), 1)
    regs = list(regs)
    for bit in (1, 2, 4, 8):
        upper = (lane & (8 * bit)) != 0
        for i in range(16):
            if i & bit:
                continue
            low, high = regs[i], regs[i | bit]
            regs[i] = jnp.where(upper, pltpu.roll(high, 8 * bit, 1), low)
            regs[i | bit] = jnp.where(upper, high, pltpu.roll(low, LANES - 8 * bit, 1))
    return regs


def row_of(part, y):
    return (y // 4) * 8 + part * 4 + y % 4


def params(mib=20):
    return pltpu.CompilerParams(vmem_limit_bytes=mib << 20)


def hbm(*arrays):
    return [pltpu.with_memory_space_constraint(x, pltpu.HBM) for x in arrays]


def cost(flops, moved):
    return pl.CostEstimate(flops=flops, bytes_accessed=moved, transcendentals=0)


def pack_input_kernel(in_ref, out_ref, field, wire, in_sems, out_sems):
    copies = []
    for j in range(3):
        rows = pl.ds(j * LANES, LANES)
        copies.append(pltpu.make_async_copy(in_ref.at[rows], field.at[rows], in_sems.at[j]))
        copies[-1].start()
    out = []
    for j in range(3):
        copies[j].wait()
        for tile in range(COLS):
            lanes = slice(tile * LANES, (tile + 1) * LANES)
            block = field[j * LANES : (j + 1) * LANES, lanes]
            wire[pl.ds(tile * ROWS + j, LANES, stride=3), :] = block.T
            if j == 2 and tile % 3 == 2:
                rows = pl.ds((tile - 2) * ROWS, 3 * ROWS)
                copy = pltpu.make_async_copy(
                    wire.at[rows], out_ref.at[rows], out_sems.at[tile // 3]
                )
                copy.start()
                out.append(copy)
    for copy in out:
        copy.wait()


def pack_input(wave):
    return pl.pallas_call(
        pack_input_kernel,
        out_shape=SENT,
        in_specs=[HBM],
        out_specs=HBM,
        scratch_shapes=[
            pltpu.VMEM((ROWS, NR), jnp.float32),
            pltpu.VMEM((WIRE, LANES), jnp.float32),
            pltpu.SemaphoreType.DMA((3,)),
            pltpu.SemaphoreType.DMA((4,)),
        ],
        compiler_params=params(12),
        name="pack_input",
    )(*hbm(wave))


def order_operator_kernel(in_ref, high_ref, low_ref, held):
    step = pl.program_id(0)

    @pl.when(step < COLS)
    def _():
        for y in range(COLS):
            block = in_ref[pl.ds(y, LANES, stride=COLS), :].T
            held[y, pl.ds(pl.multiple_of(step * LANES, LANES), LANES), :] = block

    @pl.when(step >= COLS)
    def _():
        y = step - COLS
        for ya in range(COLS):
            block = held[y, pl.ds(ya, LANES, stride=COLS), :]
            high = block.astype(jnp.bfloat16)
            rows = slice(ya * LANES, (ya + 1) * LANES)
            high_ref[0, rows, :] = high
            low_ref[0, rows, :] = (block - high.astype(jnp.float32)).astype(jnp.bfloat16)


def order_operator(radial_op):
    out = pltpu.HBM((COLS, NR, LANES), jnp.bfloat16)
    spec = pl.BlockSpec((1, NR, LANES), lambda i: (jnp.maximum(i - COLS, 0), 0, 0))
    return pl.pallas_call(
        order_operator_kernel,
        out_shape=(out, out),
        grid=(2 * COLS,),
        in_specs=[pl.BlockSpec((NR, LANES), lambda i: (0, jnp.minimum(i, COLS - 1)))],
        out_specs=(spec, spec),
        scratch_shapes=[pltpu.VMEM((COLS, NR, LANES), jnp.float32)],
        compiler_params=params(),
        cost_estimate=cost(1 << 24, 4 * NR * NR * 2),
        name="order_operator",
    )(*hbm(radial_op))


def split_terms(tiles_ref, high, low):
    for tile in range(COLS):
        block = tiles_ref[tile]
        upper = block.astype(jnp.bfloat16)
        high[:, tile * LANES : (tile + 1) * LANES] = upper
        low[:, tile * LANES : (tile + 1) * LANES] = (
            block - upper.astype(jnp.float32)
        ).astype(jnp.bfloat16)


def operator_copies(op_high_ref, op_low_ref, op_high, op_low, sems):
    copies = []
    for turn in range(TURNS):
        tiles = pl.ds(turn * TURN, TURN)
        for k, (src, dst) in enumerate(((op_high_ref, op_high), (op_low_ref, op_low))):
            copies.append(
                pltpu.make_async_copy(src.at[tiles], dst.at[tiles], sems.at[2 * turn + k])
            )
    return copies


def pack_image(tiles, image, wire):
    for tile in tiles:
        for j in range(3):
            regs = [image[tile, 24 * c + 8 * j : 24 * c + 8 * j + 8, :] for c in range(CH)]
            rows = pl.ds(tile * 3 + j, LANES, stride=EACH)
            wire[rows, :] = jnp.concatenate(regs, axis=0).T


def radial_image(copies, high, low, op_high, op_low, image, image_ref, wire, wire_ref, sems):
    out = []
    for turn in range(TURNS):
        tiles = range(turn * TURN, (turn + 1) * TURN)
        copies[2 * turn].wait()
        copies[2 * turn + 1].wait()
        upper = jnp.concatenate([op_high[i] for i in tiles], axis=1)
        lower = jnp.concatenate([op_low[i] for i in tiles], axis=1)
        total = jnp.dot(high[...], upper, preferred_element_type=jnp.float32)
        total += jnp.dot(low[...], upper, preferred_element_type=jnp.float32)
        total += jnp.dot(high[...], lower, preferred_element_type=jnp.float32)
        for i, tile in enumerate(tiles):
            image[tile] = total[:, i * LANES : (i + 1) * LANES]
        if turn > 0:
            pack_image(range((turn - 1) * TURN, turn * TURN), image, wire)
        part = pl.ds(turn * TURN, TURN)
        out.append(pltpu.make_async_copy(image.at[part], image_ref.at[part], sems.at[turn]))
        out[-1].start()
    pack_image(range((TURNS - 1) * TURN, COLS), image, wire)
    out.append(pltpu.make_async_copy(wire, wire_ref, sems.at[TURNS]))
    out[-1].start()
    for copy in out:
        copy.wait()


def unpack_input(recv_ref, field_ref, held):
    for s in range(STR):
        for j in range(3):
            rows = [
                recv_ref[pl.ds(s * EACH + y * 3 + j, 8, stride=STR * EACH), :]
                for y in range(COLS)
            ]
            start = s * ROWS + j * LANES
            held[start : start + LANES, :96] = jnp.concatenate(rows, axis=0).T
    for pc in range(4):
        for ya in range(COLS):
            rows = [
                held[pl.ds(s * ROWS + pc * 96 + ya, 8, stride=COLS), :] for s in range(STR)
            ]
            block = jnp.concatenate(rows, axis=0).T
            for y in range(COLS):
                start = (pc % 2) * 24 + row_of(pc // 2, y)
                field_ref[ya, pl.ds(start, 8, stride=48), :] = block[8 * y : 8 * y + 8, :]


def first_image_kernel(
    recv_ref,
    op_high_ref,
    op_low_ref,
    field_ref,
    image_ref,
    wire_ref,
    high,
    low,
    op_high,
    op_low,
    image,
    wire,
    op_sems,
    out_sems,
    held,
    field,
    sem,
):
    copies = operator_copies(op_high_ref, op_low_ref, op_high, op_low, op_sems)
    for copy in copies:
        copy.start()
    unpack_input(recv_ref, field, held)
    keep = pltpu.make_async_copy(field, field_ref, sem)
    keep.start()
    split_terms(field, high, low)
    radial_image(
        copies, high, low, op_high, op_low, image, image_ref, wire, wire_ref, out_sems
    )
    keep.wait()


def first_image(recv, op_high, op_low):
    return pl.pallas_call(
        first_image_kernel,
        out_shape=(TILES, TILES, SENT),
        in_specs=[VMEM, HBM, HBM],
        out_specs=(HBM, HBM, HBM),
        scratch_shapes=PRODUCT_SCRATCH
        + [
            pltpu.VMEM((STR * ROWS, LANES), jnp.float32),
            HELD,
            pltpu.SemaphoreType.DMA,
        ],
        compiler_params=params(36),
        cost_estimate=cost(FLOPS, 20 << 20),
        name="first_image",
    )(recv, *hbm(op_high, op_low))


def position_of(step, device):
    lane = lax.broadcasted_iota(jnp.int32, (24, LANES), 1)
    row = lax.broadcasted_iota(jnp.int32, (24, LANES), 0)
    return 12 * lane + step, 12 * device + (row // 8) * 4 + row % 4


def couple_kernel(device_ref, coupling_ref, couple_ref, field_ref, image_ref, out_ref, turned):
    step = pl.program_id(0)
    a, b = position_of(step, device_ref[0])
    first = a.astype(jnp.float32) * (8.0 / NR)
    second = b.astype(jnp.float32) * (8.0 / NR)
    greater = jnp.maximum(first, second)
    inverse = 1.0 / jnp.sqrt(greater * greater + 1.0)
    ratio = jnp.minimum(first, second) * inverse
    row = lax.broadcasted_iota(jnp.int32, (8, LANES), 0)
    sign = jnp.where(row < 4, -1.0, 1.0)
    for c in range(CH):
        for t in range(3):
            block = field_ref[0, c, 8 * t : 8 * t + 8, :]
            turned[c, 8 * t : 8 * t + 8, :] = pltpu.roll(block, 4, 0) * sign

    @pl.loop(0, CH)
    def _(c):
        total = jnp.zeros((24, LANES), jnp.float32)
        for order in reversed(range(MULT)):
            source = couple_ref[c, order]
            term = coupling_ref[0, c, order] * field_ref[0, source]
            term += coupling_ref[1, c, order] * turned[source]
            total = total * ratio + term
        out_ref[0, c] = image_ref[0, c] + total * inverse


def couple_terms(device, coupling, couple, field, image):
    shape = (COLS, CH, 24, LANES)
    spec = pl.BlockSpec((1,) + shape[1:], lambda i: (i, 0, 0, 0))
    out = pl.pallas_call(
        couple_kernel,
        out_shape=pltpu.HBM(shape, jnp.float32),
        grid=(COLS,),
        in_specs=[SMEM, SMEM, SMEM, spec, spec],
        out_specs=spec,
        scratch_shapes=[pltpu.VMEM((CH, 24, LANES), jnp.float32)],
        compiler_params=params(6),
        cost_estimate=cost(1 << 28, 8 << 20),
        name="couple_terms",
    )(device, coupling, couple, *hbm(field.reshape(shape), image.reshape(shape)))
    return out.reshape(TILES.shape)


def unpack_mirror(recv_ref, mirror, block):
    for y in range(COLS):
        for j in range(3):
            block[...] = recv_ref[pl.ds(y * 3 + j, LANES, stride=EACH), :].T
            for part in range(2):
                for k in range(4):
                    mirror[4 * j + k, pl.ds(row_of(part, y), CH, stride=24), :] = block[
                        pl.ds(part * 4 + k, CH, stride=8), :
                    ]


def live_sums(pair, device_ref, partner_ref, extent_ref, direct_ref, mirror, use):
    here = pl.ds(pl.multiple_of(pair * 48, 16), 48)
    lane = 12 * lax.broadcasted_iota(jnp.int32, (48, LANES), 1)
    _, b = position_of(0, device_ref[0])
    reach, there = [], []
    for c in range(2):
        extent = extent_ref[pair * 2 + c]
        partner = partner_ref[pair * 2 + c]
        reach.append(jnp.where(b < extent, extent, 0))
        there.append(pl.ds(pl.multiple_of(partner * 24, 8), 24))
    reach = jnp.concatenate(reach, axis=0) - lane
    for tile in range(COLS):
        other = jnp.concatenate([mirror[tile, rows, :] for rows in there], axis=0)
        total = direct_ref[tile, here, :] + other
        use(tile, here, jnp.where(reach > tile, total, 0.0))


def second_image_kernel(
    device_ref,
    partner_ref,
    extent_ref,
    recv_ref,
    direct_ref,
    op_high_ref,
    op_low_ref,
    field_ref,
    image_ref,
    wire_ref,
    high,
    low,
    op_high,
    op_low,
    image,
    wire,
    op_sems,
    out_sems,
    mirror,
    block,
    direct,
    field,
    sems,
):
    fetch = pltpu.make_async_copy(direct_ref, direct, sems.at[0])
    fetch.start()
    copies = operator_copies(op_high_ref, op_low_ref, op_high, op_low, op_sems)
    for copy in copies:
        copy.start()
    unpack_mirror(recv_ref, mirror, block)
    fetch.wait()

    def use(tile, here, total):
        field[tile, here, :] = total
        lanes = slice(tile * LANES, (tile + 1) * LANES)
        upper = total.astype(jnp.bfloat16)
        high[here, lanes] = upper
        low[here, lanes] = (total - upper.astype(jnp.float32)).astype(jnp.bfloat16)

    @pl.loop(0, CH // 2)
    def _(pair):
        live_sums(pair, device_ref, partner_ref, extent_ref, direct, mirror, use)

    keep = pltpu.make_async_copy(field, field_ref, sems.at[1])
    keep.start()
    radial_image(
        copies, high, low, op_high, op_low, image, image_ref, wire, wire_ref, out_sems
    )
    keep.wait()


def second_image(device, partner, extent, recv, direct, op_high, op_low):
    return pl.pallas_call(
        second_image_kernel,
        out_shape=(TILES, TILES, SENT),
        in_specs=[SMEM, SMEM, SMEM, VMEM, HBM, HBM, HBM],
        out_specs=(HBM, HBM, HBM),
        scratch_shapes=PRODUCT_SCRATCH
        + [
            HELD,
            pltpu.VMEM((LANES, LANES), jnp.float32),
            HELD,
            HELD,
            pltpu.SemaphoreType.DMA((2,)),
        ],
        compiler_params=params(36),
        cost_estimate=cost(FLOPS, 25 << 20),
        name="second_image",
    )(device, partner, extent, recv, *hbm(direct, op_high, op_low))


def pack_first_kernel(field_ref, wire_ref):
    for tile in range(COLS):
        for k in range(3):
            block = field_ref[tile, k * LANES : (k + 1) * LANES, :].T
            for s in range(STR):
                start = s * 288 + k * 96 + tile
                wire_ref[pl.ds(start, 8, stride=COLS), :] = block[8 * s : 8 * s + 8, :]


def pack_first(field):
    return pl.pallas_call(
        pack_first_kernel,
        out_shape=SENT,
        grid=(1,),
        in_specs=[TILES_SPEC],
        out_specs=SENT_SPEC,
        compiler_params=params(12),
        cost_estimate=cost(1 << 24, 5 << 20),
        name="pack_first",
    )(*hbm(field))


def place_first_kernel(recv_ref, out_ref, rows):
    for s in range(STR):
        for k in range(3):
            start = s * 288 + k * 96
            block = recv_ref[start : start + 96, :].T
            for i in range(16):
                c, t = divmod(16 * k + i, 3)
                for part in range(2):
                    at = 8 * i + 4 * part
                    rows[part * CH + c, 12 * s + 4 * t : 12 * s + 4 * t + 4, :] = block[
                        at : at + 4, :
                    ]
    for i in range(2 * CH):
        out_ref[i] = rows[i].T


def place_first(recv):
    out = pl.pallas_call(
        place_first_kernel,
        out_shape=jax.ShapeDtypeStruct((2 * CH, 96, 192), jnp.float32),
        grid=(1,),
        in_specs=[SENT_SPEC],
        out_specs=pl.BlockSpec((2 * CH, 96, 192), lambda i: (0, 0, 0)),
        scratch_shapes=[pltpu.VMEM((2 * CH, 192, 96), jnp.float32)],
        compiler_params=params(24),
        cost_estimate=cost(1 << 24, 5 << 20),
        name="place_first",
    )(*hbm(recv))
    return out.reshape(2, CH, 96, 192)


def second_vector_kernel(
    device_ref,
    partner_ref,
    extent_ref,
    recv_ref,
    direct_ref,
    field_ref,
    output_ref,
    mirror,
    result,
    block,
):
    unpack_mirror(recv_ref, mirror, block)

    def keep(tile, here, total):
        result[tile, here, :] = 2.0 * total - field_ref[tile, here, :]

    @pl.loop(0, CH // 2)
    def _(pair):
        live_sums(pair, device_ref, partner_ref, extent_ref, direct_ref, mirror, keep)

    for tile in range(COLS):
        for t in range(3):
            regs = swap_groups(
                result[tile, 24 * c + 8 * t : 24 * c + 8 * t + 8, :] for c in range(CH)
            )
            for s in range(STR):
                start = s * 288 + tile * 24 + t * 8
                output_ref[start : start + 8, :] = regs[s]


def second_vector(device, partner, extent, recv, direct, field):
    return pl.pallas_call(
        second_vector_kernel,
        out_shape=SENT,
        grid=(1,),
        in_specs=[SMEM, SMEM, SMEM, VMEM, TILES_SPEC, TILES_SPEC],
        out_specs=SENT_SPEC,
        scratch_shapes=[HELD, HELD, pltpu.VMEM((LANES, LANES), jnp.float32)],
        compiler_params=params(32),
        cost_estimate=cost(1 << 24, 10 << 20),
        name="second_vector",
    )(device, partner, extent, recv, *hbm(direct, field))


def place_output_kernel(recv_ref, out_ref, rows, left, right):
    part = pl.program_id(0)
    for ya in range(COLS):
        for s in range(STR):
            for t in range(3):
                start = s * 288 + ya * 24 + t * 8
                block = recv_ref[start : start + 8, :]
                block = jnp.where(part == 0, block[:4], block[4:])
                rows[12 * s + 4 * t : 12 * s + 4 * t + 4, :] = block
        turned = rows[...].T
        left[pl.ds(ya, LANES, stride=COLS), :] = turned[:, :LANES]
        right[pl.ds(ya, LANES, stride=COLS), :] = turned[:, LANES:]
    out_ref[0, :, :LANES] = left[...]
    out_ref[0, :, LANES:] = right[:, :64]


def place_output(recv):
    out = pl.pallas_call(
        place_output_kernel,
        out_shape=jax.ShapeDtypeStruct((2, NR, 192), jnp.float32),
        grid=(2,),
        in_specs=[VMEM],
        out_specs=pl.BlockSpec((1, NR, 192), lambda i: (i, 0, 0)),
        scratch_shapes=[
            pltpu.VMEM((256, LANES), jnp.float32),
            pltpu.VMEM((NR, LANES), jnp.float32),
            pltpu.VMEM((NR, LANES), jnp.float32),
        ],
        compiler_params=params(20),
        cost_estimate=cost(1 << 24, 5 << 20),
        name="place_output",
    )(recv)
    return out.reshape(2, CH, 96, 192)


def exchange_all(sent):
    sent = sent.reshape(DEV, 9, 4, LANES)
    recv = lax.all_to_all(sent, ("chan", "strip"), 0, 0, tiled=True)
    return recv.reshape(WIRE, LANES)


def exchange_strip(sent):
    sent = sent.reshape(STR, WIRE // STR, LANES)
    return lax.all_to_all(sent, "strip", 0, 0, tiled=True).reshape(WIRE, LANES)


def local(wave_field, radial_op, coupling, couple, partner, extent):
    device = (lax.axis_index("chan") * STR + lax.axis_index("strip")).reshape(1)
    op_high, op_low = order_operator(radial_op)
    recv = exchange_all(pack_input(wave_field.reshape(ROWS, NR)))
    field, image, sent = first_image(recv, op_high, op_low)
    recv = exchange_all(sent)
    direct = couple_terms(device, coupling, couple, field, image)
    first, image, sent = second_image(
        device, partner, extent, recv, direct, op_high, op_low
    )
    recv = exchange_all(sent)
    direct = couple_terms(device, coupling, couple, first, image)
    first_step = place_first(exchange_strip(pack_first(first)))
    output = second_vector(device, partner, extent, recv, direct, field)
    second_step = place_output(exchange_strip(output))
    return (first_step, second_step)


def solution(mesh):
    placed = (P(None, "chan", "strip", None), P(), P(), P(), P(), P())
    return jax.shard_map(
        local,
        mesh=mesh,
        in_specs=placed,
        out_specs=(P(None, None, "strip", "chan"), P(None, None, "strip", "chan")),
        check_vma=False,
    )
```

```python
import functools

import jax
import jax.numpy as jnp
from jax import lax
from jax.experimental import pallas as pl
from jax.experimental.pallas import tpu as pltpu
from jax.sharding import PartitionSpec as P

NR = 1536
CH = 16
MULT = 8
DEV = 128
GRP = 8
STR = 16
COLS = 12
LANES = 128
ROWS = 384
WIRE = 4608
EACH = 36


TILES = pltpu.HBM((COLS, ROWS, LANES), jnp.float32)
SENT = pltpu.HBM((WIRE, LANES), jnp.float32)
SMEM = pl.BlockSpec(memory_space=pltpu.SMEM)
HBM = pl.BlockSpec(memory_space=pltpu.HBM)
VMEM = pl.BlockSpec(memory_space=pltpu.VMEM)
SENT_SPEC = pl.BlockSpec((WIRE, LANES), lambda i: (0, 0))
TILES_SPEC = pl.BlockSpec((COLS, ROWS, LANES), lambda i: (0, 0, 0))
HELD = pltpu.VMEM((COLS, ROWS, LANES), jnp.float32)
TURN = 4
TURNS = COLS // TURN
PRODUCT_SCRATCH = [
    pltpu.VMEM((ROWS, NR), jnp.bfloat16),
    pltpu.VMEM((ROWS, NR), jnp.bfloat16),
    pltpu.VMEM((COLS, NR, LANES), jnp.bfloat16),
    pltpu.VMEM((COLS, NR, LANES), jnp.bfloat16),
    HELD,
    pltpu.VMEM((WIRE, LANES), jnp.float32),
    pltpu.SemaphoreType.DMA((2 * TURNS,)),
    pltpu.SemaphoreType.DMA((TURNS + 1,)),
]
FLOPS = 2 * 3 * ROWS * NR * NR


def swap_groups(regs):
    lane = lax.broadcasted_iota(jnp.int32, (8, LANES), 1)
    regs = list(regs)
    for bit in (1, 2, 4, 8):
        upper = (lane & (8 * bit)) != 0
        for i in range(16):
            if i & bit:
                continue
            low, high = regs[i], regs[i | bit]
            regs[i] = jnp.where(upper, pltpu.roll(high, 8 * bit, 1), low)
            regs[i | bit] = jnp.where(upper, high, pltpu.roll(low, LANES - 8 * bit, 1))
    return regs


def row_of(part, y):
    return (y // 4) * 8 + part * 4 + y % 4


def params(mib=20):
    return pltpu.CompilerParams(vmem_limit_bytes=mib << 20)


def hbm(*arrays):
    return [pltpu.with_memory_space_constraint(x, pltpu.HBM) for x in arrays]


def cost(flops, moved):
    return pl.CostEstimate(flops=flops, bytes_accessed=moved, transcendentals=0)


def pack_input_kernel(in_ref, out_ref, field, wire, in_sems, out_sems):
    copies = []
    for k in range(4):
        part = pl.ds(k * 3 * LANES, 3 * LANES)
        copies.append(
            pltpu.make_async_copy(in_ref.at[:, part], field.at[:, part], in_sems.at[k])
        )
        copies[-1].start()
    out = []
    for k in range(4):
        copies[k].wait()
        for tile in range(3 * k, 3 * k + 3):
            for j in range(3):
                lanes = slice(tile * LANES, (tile + 1) * LANES)
                block = field[j * LANES : (j + 1) * LANES, lanes]
                wire[pl.ds(tile * ROWS + j, LANES, stride=3), :] = block.T
        rows = pl.ds(k * 3 * ROWS, 3 * ROWS)
        out.append(pltpu.make_async_copy(wire.at[rows], out_ref.at[rows], out_sems.at[k]))
        out[-1].start()
    for copy in out:
        copy.wait()


def pack_input(wave):
    return pl.pallas_call(
        pack_input_kernel,
        out_shape=SENT,
        in_specs=[HBM],
        out_specs=HBM,
        scratch_shapes=[
            pltpu.VMEM((ROWS, NR), jnp.float32),
            pltpu.VMEM((WIRE, LANES), jnp.float32),
            pltpu.SemaphoreType.DMA((4,)),
            pltpu.SemaphoreType.DMA((4,)),
        ],
        compiler_params=params(12),
        name="pack_input",
    )(*hbm(wave))


def order_operator_kernel(in_ref, high_ref, low_ref, held):
    step = pl.program_id(0)

    @pl.when(step < COLS)
    def _():
        for y in range(COLS):
            block = in_ref[pl.ds(y, LANES, stride=COLS), :].T
            held[y, pl.ds(pl.multiple_of(step * LANES, LANES), LANES), :] = block

    @pl.when(step >= COLS)
    def _():
        y = step - COLS
        for ya in range(COLS):
            block = held[y, pl.ds(ya, LANES, stride=COLS), :]
            high = block.astype(jnp.bfloat16)
            rows = slice(ya * LANES, (ya + 1) * LANES)
            high_ref[0, rows, :] = high
            low_ref[0, rows, :] = (block - high.astype(jnp.float32)).astype(jnp.bfloat16)


def order_operator(radial_op):
    out = pltpu.HBM((COLS, NR, LANES), jnp.bfloat16)
    spec = pl.BlockSpec((1, NR, LANES), lambda i: (jnp.maximum(i - COLS, 0), 0, 0))
    return pl.pallas_call(
        order_operator_kernel,
        out_shape=(out, out),
        grid=(2 * COLS,),
        in_specs=[pl.BlockSpec((NR, LANES), lambda i: (0, jnp.minimum(i, COLS - 1)))],
        out_specs=(spec, spec),
        scratch_shapes=[pltpu.VMEM((COLS, NR, LANES), jnp.float32)],
        compiler_params=params(),
        cost_estimate=cost(1 << 24, 4 * NR * NR * 2),
        name="order_operator",
    )(*hbm(radial_op))


def split_terms(block, tile, rows, high, low):
    lanes = slice(tile * LANES, (tile + 1) * LANES)
    upper = block.astype(jnp.bfloat16)
    high[rows, lanes] = upper
    low[rows, lanes] = (block - upper.astype(jnp.float32)).astype(jnp.bfloat16)


def operator_copies(op_high_ref, op_low_ref, op_high, op_low, sems):
    copies = []
    for turn in range(TURNS):
        tiles = pl.ds(turn * TURN, TURN)
        for k, (src, dst) in enumerate(((op_high_ref, op_high), (op_low_ref, op_low))):
            copies.append(
                pltpu.make_async_copy(src.at[tiles], dst.at[tiles], sems.at[2 * turn + k])
            )
    return copies


def pack_image(tiles, image, wire):
    for tile in tiles:
        for j in range(3):
            regs = [image[tile, 24 * c + 8 * j : 24 * c + 8 * j + 8, :] for c in range(CH)]
            rows = pl.ds(tile * 3 + j, LANES, stride=EACH)
            wire[rows, :] = jnp.concatenate(regs, axis=0).T


def radial_image(copies, high, low, op_high, op_low, image, image_ref, wire, wire_ref, sems):
    out = []
    for turn in range(TURNS):
        tiles = range(turn * TURN, (turn + 1) * TURN)
        copies[2 * turn].wait()
        copies[2 * turn + 1].wait()
        upper = jnp.concatenate([op_high[i] for i in tiles], axis=1)
        lower = jnp.concatenate([op_low[i] for i in tiles], axis=1)
        total = jnp.dot(high[...], upper, preferred_element_type=jnp.float32)
        total += jnp.dot(low[...], upper, preferred_element_type=jnp.float32)
        total += jnp.dot(high[...], lower, preferred_element_type=jnp.float32)
        for i, tile in enumerate(tiles):
            image[tile] = total[:, i * LANES : (i + 1) * LANES]
        if turn > 0:
            pack_image(range((turn - 1) * TURN, turn * TURN), image, wire)
        part = pl.ds(turn * TURN, TURN)
        out.append(pltpu.make_async_copy(image.at[part], image_ref.at[part], sems.at[turn]))
        out[-1].start()
    pack_image(range((TURNS - 1) * TURN, COLS), image, wire)
    out.append(pltpu.make_async_copy(wire, wire_ref, sems.at[TURNS]))
    out[-1].start()
    for copy in out:
        copy.wait()


def unpack_input(recv_ref, field_ref, held, high, low):
    for s in range(STR):
        for j in range(3):
            rows = [
                recv_ref[pl.ds(s * EACH + y * 3 + j, 8, stride=STR * EACH), :]
                for y in range(COLS)
            ]
            start = s * ROWS + j * LANES
            held[start : start + LANES, :96] = jnp.concatenate(rows, axis=0).T
    for ya in range(COLS):
        for pc in range(4):
            rows = [
                held[pl.ds(s * ROWS + pc * 96 + ya, 8, stride=COLS), :] for s in range(STR)
            ]
            block = jnp.concatenate(rows, axis=0).T
            for y in range(COLS):
                start = (pc % 2) * 24 + row_of(pc // 2, y)
                field_ref[ya, pl.ds(start, 8, stride=48), :] = block[8 * y : 8 * y + 8, :]
        split_terms(field_ref[ya], ya, slice(0, ROWS), high, low)


def first_image_kernel(
    recv_ref,
    op_high_ref,
    op_low_ref,
    field_ref,
    image_ref,
    wire_ref,
    high,
    low,
    op_high,
    op_low,
    image,
    wire,
    op_sems,
    out_sems,
    held,
    field,
    sem,
):
    copies = operator_copies(op_high_ref, op_low_ref, op_high, op_low, op_sems)
    for copy in copies:
        copy.start()
    unpack_input(recv_ref, field, held, high, low)
    keep = pltpu.make_async_copy(field, field_ref, sem)
    keep.start()
    radial_image(
        copies, high, low, op_high, op_low, image, image_ref, wire, wire_ref, out_sems
    )
    keep.wait()


def first_image(recv, op_high, op_low):
    return pl.pallas_call(
        first_image_kernel,
        out_shape=(TILES, TILES, SENT),
        in_specs=[VMEM, HBM, HBM],
        out_specs=(HBM, HBM, HBM),
        scratch_shapes=PRODUCT_SCRATCH
        + [
            pltpu.VMEM((STR * ROWS, LANES), jnp.float32),
            HELD,
            pltpu.SemaphoreType.DMA,
        ],
        compiler_params=params(36),
        cost_estimate=cost(FLOPS, 20 << 20),
        name="first_image",
    )(recv, *hbm(op_high, op_low))


def position_of(step, device):
    lane = lax.broadcasted_iota(jnp.int32, (24, LANES), 1)
    row = lax.broadcasted_iota(jnp.int32, (24, LANES), 0)
    return 12 * lane + step, 12 * device + (row // 8) * 4 + row % 4


def couple_kernel(device_ref, coupling_ref, couple_ref, field_ref, image_ref, out_ref, turned):
    step = pl.program_id(0)
    a, b = position_of(step, device_ref[0])
    first = a.astype(jnp.float32) * (8.0 / NR)
    second = b.astype(jnp.float32) * (8.0 / NR)
    greater = jnp.maximum(first, second)
    inverse = 1.0 / jnp.sqrt(greater * greater + 1.0)
    ratio = jnp.minimum(first, second) * inverse
    row = lax.broadcasted_iota(jnp.int32, (8, LANES), 0)
    sign = jnp.where(row < 4, -1.0, 1.0)
    for c in range(CH):
        for t in range(3):
            block = field_ref[0, c, 8 * t : 8 * t + 8, :]
            turned[c, 8 * t : 8 * t + 8, :] = pltpu.roll(block, 4, 0) * sign

    @pl.loop(0, CH)
    def _(c):
        total = jnp.zeros((24, LANES), jnp.float32)
        for order in reversed(range(MULT)):
            source = couple_ref[c, order]
            term = coupling_ref[0, c, order] * field_ref[0, source]
            term += coupling_ref[1, c, order] * turned[source]
            total = total * ratio + term
        out_ref[0, c] = image_ref[0, c] + total * inverse


def couple_terms(device, coupling, couple, field, image):
    shape = (COLS, CH, 24, LANES)
    spec = pl.BlockSpec((1,) + shape[1:], lambda i: (i, 0, 0, 0))
    out = pl.pallas_call(
        couple_kernel,
        out_shape=pltpu.HBM(shape, jnp.float32),
        grid=(COLS,),
        in_specs=[SMEM, SMEM, SMEM, spec, spec],
        out_specs=spec,
        scratch_shapes=[pltpu.VMEM((CH, 24, LANES), jnp.float32)],
        compiler_params=params(6),
        cost_estimate=cost(1 << 28, 8 << 20),
        name="couple_terms",
    )(device, coupling, couple, *hbm(field.reshape(shape), image.reshape(shape)))
    return out.reshape(TILES.shape)


def unpack_mirror(recv_ref, mirror, block):
    for y in range(COLS):
        for j in range(3):
            block[...] = recv_ref[pl.ds(y * 3 + j, LANES, stride=EACH), :].T
            for part in range(2):
                for k in range(4):
                    mirror[4 * j + k, pl.ds(row_of(part, y), CH, stride=24), :] = block[
                        pl.ds(part * 4 + k, CH, stride=8), :
                    ]


def live_sums(pair, device_ref, partner_ref, extent_ref, direct_ref, mirror, use):
    here = pl.ds(pl.multiple_of(pair * 48, 16), 48)
    lane = 12 * lax.broadcasted_iota(jnp.int32, (48, LANES), 1)
    _, b = position_of(0, device_ref[0])
    reach, there = [], []
    for c in range(2):
        extent = extent_ref[pair * 2 + c]
        partner = partner_ref[pair * 2 + c]
        reach.append(jnp.where(b < extent, extent, 0))
        there.append(pl.ds(pl.multiple_of(partner * 24, 8), 24))
    reach = jnp.concatenate(reach, axis=0) - lane
    for tile in range(COLS):
        other = jnp.concatenate([mirror[tile, rows, :] for rows in there], axis=0)
        total = direct_ref[tile, here, :] + other
        use(tile, here, jnp.where(reach > tile, total, 0.0))


def second_image_kernel(
    device_ref,
    partner_ref,
    extent_ref,
    recv_ref,
    direct_ref,
    op_high_ref,
    op_low_ref,
    field_ref,
    image_ref,
    wire_ref,
    high,
    low,
    op_high,
    op_low,
    image,
    wire,
    op_sems,
    out_sems,
    mirror,
    block,
    direct,
    field,
    sems,
):
    fetch = pltpu.make_async_copy(direct_ref, direct, sems.at[0])
    fetch.start()
    copies = operator_copies(op_high_ref, op_low_ref, op_high, op_low, op_sems)
    for copy in copies:
        copy.start()
    unpack_mirror(recv_ref, mirror, block)
    fetch.wait()

    def use(tile, here, total):
        field[tile, here, :] = total
        split_terms(total, tile, here, high, low)

    @pl.loop(0, CH // 2)
    def _(pair):
        live_sums(pair, device_ref, partner_ref, extent_ref, direct, mirror, use)

    keep = pltpu.make_async_copy(field, field_ref, sems.at[1])
    keep.start()
    radial_image(
        copies, high, low, op_high, op_low, image, image_ref, wire, wire_ref, out_sems
    )
    keep.wait()


def second_image(device, partner, extent, recv, direct, op_high, op_low):
    return pl.pallas_call(
        second_image_kernel,
        out_shape=(TILES, TILES, SENT),
        in_specs=[SMEM, SMEM, SMEM, VMEM, HBM, HBM, HBM],
        out_specs=(HBM, HBM, HBM),
        scratch_shapes=PRODUCT_SCRATCH
        + [
            HELD,
            pltpu.VMEM((LANES, LANES), jnp.float32),
            HELD,
            HELD,
            pltpu.SemaphoreType.DMA((2,)),
        ],
        compiler_params=params(36),
        cost_estimate=cost(FLOPS, 25 << 20),
        name="second_image",
    )(device, partner, extent, recv, *hbm(direct, op_high, op_low))


def pack_first_kernel(field_ref, wire_ref):
    for tile in range(COLS):
        for k in range(3):
            block = field_ref[tile, k * LANES : (k + 1) * LANES, :].T
            for s in range(STR):
                start = s * 288 + k * 96 + tile
                wire_ref[pl.ds(start, 8, stride=COLS), :] = block[8 * s : 8 * s + 8, :]


def pack_first(field):
    return pl.pallas_call(
        pack_first_kernel,
        out_shape=SENT,
        grid=(1,),
        in_specs=[TILES_SPEC],
        out_specs=SENT_SPEC,
        compiler_params=params(12),
        cost_estimate=cost(1 << 24, 5 << 20),
        name="pack_first",
    )(*hbm(field))


def place_first_kernel(recv_ref, out_ref, rows):
    for s in range(STR):
        for k in range(3):
            start = s * 288 + k * 96
            block = recv_ref[start : start + 96, :].T
            for i in range(16):
                c, t = divmod(16 * k + i, 3)
                for part in range(2):
                    at = 8 * i + 4 * part
                    rows[part * CH + c, 12 * s + 4 * t : 12 * s + 4 * t + 4, :] = block[
                        at : at + 4, :
                    ]
    for i in range(2 * CH):
        out_ref[i] = rows[i].T


def place_first(recv):
    out = pl.pallas_call(
        place_first_kernel,
        out_shape=jax.ShapeDtypeStruct((2 * CH, 96, 192), jnp.float32),
        grid=(1,),
        in_specs=[SENT_SPEC],
        out_specs=pl.BlockSpec((2 * CH, 96, 192), lambda i: (0, 0, 0)),
        scratch_shapes=[pltpu.VMEM((2 * CH, 192, 96), jnp.float32)],
        compiler_params=params(24),
        cost_estimate=cost(1 << 24, 5 << 20),
        name="place_first",
    )(*hbm(recv))
    return out.reshape(2, CH, 96, 192)


def second_vector_kernel(
    device_ref,
    partner_ref,
    extent_ref,
    recv_ref,
    direct_ref,
    field_ref,
    output_ref,
    mirror,
    result,
    block,
):
    unpack_mirror(recv_ref, mirror, block)

    def keep(tile, here, total):
        result[tile, here, :] = 2.0 * total - field_ref[tile, here, :]

    @pl.loop(0, CH // 2)
    def _(pair):
        live_sums(pair, device_ref, partner_ref, extent_ref, direct_ref, mirror, keep)

    for tile in range(COLS):
        for t in range(3):
            regs = swap_groups(
                result[tile, 24 * c + 8 * t : 24 * c + 8 * t + 8, :] for c in range(CH)
            )
            for s in range(STR):
                start = s * 288 + tile * 24 + t * 8
                output_ref[start : start + 8, :] = regs[s]


def second_vector(device, partner, extent, recv, direct, field):
    return pl.pallas_call(
        second_vector_kernel,
        out_shape=SENT,
        grid=(1,),
        in_specs=[SMEM, SMEM, SMEM, VMEM, TILES_SPEC, TILES_SPEC],
        out_specs=SENT_SPEC,
        scratch_shapes=[HELD, HELD, pltpu.VMEM((LANES, LANES), jnp.float32)],
        compiler_params=params(32),
        cost_estimate=cost(1 << 24, 10 << 20),
        name="second_vector",
    )(device, partner, extent, recv, *hbm(direct, field))


def place_output_kernel(recv_ref, out_ref, rows, left, right):
    part = pl.program_id(0)
    for ya in range(COLS):
        for s in range(STR):
            for t in range(3):
                start = s * 288 + ya * 24 + t * 8
                block = recv_ref[start : start + 8, :]
                block = jnp.where(part == 0, block[:4], block[4:])
                rows[12 * s + 4 * t : 12 * s + 4 * t + 4, :] = block
        turned = rows[...].T
        left[pl.ds(ya, LANES, stride=COLS), :] = turned[:, :LANES]
        right[pl.ds(ya, LANES, stride=COLS), :] = turned[:, LANES:]
    out_ref[0, :, :LANES] = left[...]
    out_ref[0, :, LANES:] = right[:, :64]


def place_output(recv):
    out = pl.pallas_call(
        place_output_kernel,
        out_shape=jax.ShapeDtypeStruct((2, NR, 192), jnp.float32),
        grid=(2,),
        in_specs=[VMEM],
        out_specs=pl.BlockSpec((1, NR, 192), lambda i: (i, 0, 0)),
        scratch_shapes=[
            pltpu.VMEM((256, LANES), jnp.float32),
            pltpu.VMEM((NR, LANES), jnp.float32),
            pltpu.VMEM((NR, LANES), jnp.float32),
        ],
        compiler_params=params(20),
        cost_estimate=cost(1 << 24, 5 << 20),
        name="place_output",
    )(recv)
    return out.reshape(2, CH, 96, 192)


def exchange_all(sent):
    sent = sent.reshape(DEV, 9, 4, LANES)
    recv = lax.all_to_all(sent, ("chan", "strip"), 0, 0, tiled=True)
    return recv.reshape(WIRE, LANES)


def exchange_strip(sent):
    sent = sent.reshape(STR, WIRE // STR, LANES)
    return lax.all_to_all(sent, "strip", 0, 0, tiled=True).reshape(WIRE, LANES)


def local(wave_field, radial_op, coupling, couple, partner, extent):
    device = (lax.axis_index("chan") * STR + lax.axis_index("strip")).reshape(1)
    op_high, op_low = order_operator(radial_op)
    recv = exchange_all(pack_input(wave_field.reshape(ROWS, NR)))
    field, image, sent = first_image(recv, op_high, op_low)
    recv = exchange_all(sent)
    direct = couple_terms(device, coupling, couple, field, image)
    first, image, sent = second_image(
        device, partner, extent, recv, direct, op_high, op_low
    )
    recv = exchange_all(sent)
    direct = couple_terms(device, coupling, couple, first, image)
    first_step = place_first(exchange_strip(pack_first(first)))
    output = second_vector(device, partner, extent, recv, direct, field)
    second_step = place_output(exchange_strip(output))
    return (first_step, second_step)


def solution(mesh):
    placed = (P(None, "chan", "strip", None), P(), P(), P(), P(), P())
    return jax.shard_map(
        local,
        mesh=mesh,
        in_specs=placed,
        out_specs=(P(None, None, "strip", "chan"), P(None, None, "strip", "chan")),
        check_vma=False,
    )
```
